512 devices in a mesh: wide: 128 (over y, z, core), narrow: 4 (over x).
Axes of the slice: x: 4, y: 8, z: 8, core: 2. Of those that a mesh axis runs over, the one named last changes fastest.
Arguments:
- queries: bfloat16 [65536, 2048], P(('wide', 'narrow')), may hold values from -8 to 8
- key_tensor: bfloat16 [65536, 256], P(('wide', 'narrow')), may hold values from -8 to 8
- value_tensor: bfloat16 [65536, 256], P(('wide', 'narrow')), may hold values from -8 to 8
- decay_logarithm: float32 [2, 65536], P(None, ('wide', 'narrow')), may hold values from -2 to 0
- lin_gain: float32 [2048], replicated, may hold values from 0.25 to 1.75
- routes: int32 [65536, 2], P(('wide', 'narrow')), may hold values from 0 to 31, all different within a row; in each aligned block of 128 rows (0 to 127, 128 to 255, ...) at most 12 rows name the same one
- route_weight: float32 [65536, 2], P(('wide', 'narrow')), may hold values from 0.2 to 1
- w_up: bfloat16 [2048, 45056], P(None, 'wide'), may hold values from -0.125 to 0.125
- w_down: bfloat16 [45056, 2048], P('wide'), may hold values from -0.15625 to 0.15625
Outputs:
- layer_out: bfloat16 [65536, 2048], P(('wide', 'narrow'))
The draws below stay inside these ranges and needn't reach their ends.
Inputs may be any that keep to these rules, and one draw needn't show every extreme that they name: `routes`: each row names 2 different experts. In each aligned block of 128 rows no expert is named more than 12 times, and in some block some expert is named exactly 12 times.
All inputs are finite; a program needn't handle non-finite values.
Results may differ from the reference program's by a relative error of at most 0.0055.
Values may be sent and summed in bfloat16 or wider, within the bound.
No kernel may reach another device: no remote copies, remote signals or barrier semaphores. Data moves between devices by JAX's collectives and lax.ppermute only.
A program may use at most 128 MiB of HBM per device.

```python
import math
import jax
import jax.numpy as jnp
import numpy as np
from jax import lax

MODEL_SPAN = 2048
QUERY_HEADS = 16
PAIRED_KV_PARTS = 2
HEAD_SIZE = 128
FF = 1408
EXPERTS = 32
TOP = 2
QUART = 4
WINDOW_KEYS = 128
DEVICE_TOKENS = 128
MOST = 12
SEGMENT_ITEMS = 65536
N_WIDE = 128
N_NARROW = 4


def attention_inputs(key):
    stochastic_seeds = jax.random.split(jax.random.fold_in(key, 23), 2)
    query_vals = jnp.clip(jax.random.normal(stochastic_seeds[0], (SEGMENT_ITEMS, MODEL_SPAN), jnp.float32), -8.0, 8.0)
    key_entries = jnp.clip(jax.random.normal(stochastic_seeds[1], (SEGMENT_ITEMS, PAIRED_KV_PARTS * HEAD_SIZE), jnp.float32), -8.0, 8.0)
    return (query_vals, key_entries)


def draw_queries(key, part):
    return attention_inputs(key)[0].astype(jnp.bfloat16)


def draw_key_tensor(key, part):
    return attention_inputs(key)[1].astype(jnp.bfloat16)


def draw_value_tensor(key, part):
    stochastic_seeds = jax.random.split(jax.random.fold_in(key, 37), 1)
    random_noise = jax.random.normal(stochastic_seeds[0], (SEGMENT_ITEMS, PAIRED_KV_PARTS * HEAD_SIZE), jnp.float32)
    return jnp.clip(random_noise, -8.0, 8.0).astype(jnp.bfloat16)


def draw_decay_logarithm(key, part):
    stochastic_seeds = jax.random.split(jax.random.fold_in(key, 11), 8)
    block_number = SEGMENT_ITEMS // DEVICE_TOKENS
    quick_count = jax.random.randint(stochastic_seeds[0], (), 1, PAIRED_KV_PARTS)
    rank_order = jax.random.permutation(stochastic_seeds[1], PAIRED_KV_PARTS)
    quick_flag = rank_order < quick_count
    gentle_rate = jnp.exp(jax.random.uniform(stochastic_seeds[2], (PAIRED_KV_PARTS,), jnp.float32, math.log(0.2), math.log(0.6))) / SEGMENT_ITEMS
    quick_rate = jnp.exp(jax.random.uniform(stochastic_seeds[3], (PAIRED_KV_PARTS,), jnp.float32, math.log(0.75), math.log(1.33))) / min(40, DEVICE_TOKENS // 2)
    base_rate = jnp.where(quick_flag, quick_rate, gentle_rate)
    block_multiplier = jnp.exp(jax.random.uniform(stochastic_seeds[4], (PAIRED_KV_PARTS, block_number), jnp.float32, math.log(0.5), math.log(2.0)))
    block_multiplier = jnp.repeat(block_multiplier, DEVICE_TOKENS, axis=1)
    coarseness = jax.random.uniform(stochastic_seeds[5], (PAIRED_KV_PARTS, SEGMENT_ITEMS), jnp.float32, 0.5, 1.5)
    fading_coefficient = -base_rate[:, None] * block_multiplier * coarseness
    spike_location = jax.random.randint(stochastic_seeds[6], (PAIRED_KV_PARTS, 2), 0, SEGMENT_ITEMS)
    spike_persistence = jax.random.uniform(stochastic_seeds[7], (PAIRED_KV_PARTS, 2), jnp.float32, 0.5, 0.8)
    equality_markers = (jnp.arange(SEGMENT_ITEMS)[None, None, :] == spike_location[:, :, None]).astype(jnp.float32)
    fading_coefficient = fading_coefficient + jnp.sum(equality_markers * jnp.log(spike_persistence)[:, :, None], axis=1)
    return fading_coefficient.astype(jnp.float32)


def levels(rng, dims, cuts, least, high):
    level = 1.0
    for axis_at, blocks in cuts:
        steps = jax.random.uniform(jax.random.fold_in(jax.random.fold_in(rng, 6), axis_at), (blocks,), jnp.float32, least / len(cuts), high / len(cuts))
        level = level * jnp.repeat(jnp.exp(steps), dims[axis_at] // blocks).reshape((-1,) + (1,) * (len(dims) - 1 - axis_at))
    return level


def assign_block(stream_key, own, number, rows, count, top, most, skew):
    sequence = jax.random.permutation(stream_key, count)
    heavy_load, ordinary = load_shares(count, rows * top, most, skew, True), load_shares(count, rows * top, most, skew, False)
    places = jnp.arange(count)

    def named(tallies, offset_by):
        used = int((tallies > 0).sum())
        fixed = max(1, used // 4)
        moved = fixed + (places - fixed + offset_by * (used - fixed)) % max(1, count - fixed)
        return jnp.zeros((count,), jnp.int32).at[sequence[jnp.where(places < fixed, places, moved)]].set(jnp.asarray(tallies, jnp.int32))

    tallies = jnp.where(number % 4 == 0, named(heavy_load, number // 4), named(ordinary, number - number // 4 - 1))
    mixed = jax.random.permutation(jax.random.fold_in(own, 3), count)
    giver, taker = mixed[0:count // 2 * 2:2], mixed[1:count // 2 * 2:2]
    slack = jnp.minimum(tallies[giver] - 1, most - tallies[taker]) // 2
    slack = jnp.where((giver == sequence[0]) | (taker == sequence[0]) | (tallies[taker] == 0), 0, jnp.maximum(slack, 0))
    moved = jax.random.randint(jax.random.fold_in(own, 4), (count // 2,), 0, 1 << 20) % (slack + 1)
    tallies = tallies.at[giver].add(-moved).at[taker].add(moved)
    items = jnp.searchsorted(jnp.cumsum(tallies), jnp.arange(rows * top), side="right").astype(jnp.int32)
    table = items.reshape(top, rows).T
    table = table[jax.random.permutation(jax.random.fold_in(own, 1), rows)]
    offset_by = jax.random.randint(jax.random.fold_in(own, 2), (rows, 1), 0, top)
    return jnp.take_along_axis(table, (jnp.arange(top)[None, :] + offset_by) % top, axis=1)


def load_shares(number_of, total, reach, slope, full):
    portions = [(1 << 20) // math.isqrt(standing ** slope) + 1 for standing in range(1, number_of + 1)]
    largest = reach if full else min(reach, max(-(-total // number_of), total * portions[0] // sum(portions)))
    least = 1 if total - largest >= number_of - 1 else 0
    counts, surplus = [largest] + [least] * (number_of - 1), total - largest - least * (number_of - 1)
    while surplus > 0:
        candidates = [i for i in range(1, number_of) if counts[i] < largest] or [i for i in range(1, number_of) if counts[i] < reach]
        whole, left = sum([portions[i] for i in candidates]), surplus
        for i in candidates:
            more = min(reach - counts[i], max(1, left * portions[i] // whole), surplus)
            counts[i] = counts[i] + more
            surplus = surplus - more
    return np.array(counts)


def gaussian(key, extent, deviation, most, cuts=(), held_as=jnp.bfloat16):
    values = jax.random.normal(key, extent, jnp.float32) * deviation
    if len(cuts) > 0:
        values = levels(key, extent, cuts, -0.22, 0.18) * values
    return jnp.clip(values, min=-most, max=most).astype(held_as)


def setup_inputs(seed: int = 0) -> dict:
    keys = jax.random.split(jax.random.key(seed), 10)
    queries = draw_queries(jax.random.fold_in(keys[9], 71), 0)
    key_tensor = draw_key_tensor(jax.random.fold_in(keys[9], 71), 0)
    value_tensor = draw_value_tensor(jax.random.fold_in(keys[9], 71), 0)
    decay_logarithm = draw_decay_logarithm(jax.random.fold_in(keys[9], 71), 0)
    lin_gain = jnp.clip(1.0 + 0.15 * jax.random.normal(keys[4], (MODEL_SPAN,), jnp.float32), 0.25, 1.75)
    routes_keys = jax.random.split(jax.random.fold_in(keys[5], 1), SEGMENT_ITEMS // DEVICE_TOKENS)
    routes_turns = jax.random.permutation(jax.random.fold_in(keys[5], 3), SEGMENT_ITEMS // DEVICE_TOKENS)
    routes = jax.vmap(lambda own, number: assign_block(jax.random.fold_in(keys[5], 2), own, number, DEVICE_TOKENS, EXPERTS, TOP, MOST, 2))(routes_keys, routes_turns).reshape((SEGMENT_ITEMS, TOP))
    route_weight = jnp.clip(0.2 + 0.8 * jax.random.uniform(keys[6], (SEGMENT_ITEMS, TOP), jnp.float32) ** levels(keys[6], (SEGMENT_ITEMS, TOP), ((0, 512),), -0.2, 0.2), 0.2, 1.0)
    w_up = gaussian(keys[7], (MODEL_SPAN, EXPERTS * FF), MODEL_SPAN ** -0.5, 0.125, ((1, 128),))
    w_down = gaussian(keys[8], (EXPERTS * FF, MODEL_SPAN), FF ** -0.5, 0.15625, ((0, 128),))
    return dict(queries=queries, key_tensor=key_tensor, value_tensor=value_tensor, decay_logarithm=decay_logarithm, lin_gain=lin_gain, routes=routes, route_weight=route_weight, w_up=w_up, w_down=w_down)


def reference(queries, key_tensor, value_tensor, decay_logarithm, lin_gain, routes, route_weight, w_up, w_down):
    group_extent = QUERY_HEADS // PAIRED_KV_PARTS
    block_length = min(512, SEGMENT_ITEMS)
    block_number = SEGMENT_ITEMS // block_length
    hi_prec = lax.Precision.HIGHEST
    scale_multiplier = HEAD_SIZE ** (-0.5)
    query_single = queries.astype(jnp.float32).reshape(block_number, block_length, PAIRED_KV_PARTS, group_extent, HEAD_SIZE)
    key_single = key_tensor.astype(jnp.float32).reshape(block_number, block_length, PAIRED_KV_PARTS, HEAD_SIZE) * scale_multiplier
    value_single = value_tensor.astype(jnp.float32).reshape(block_number, block_length, PAIRED_KV_PARTS, HEAD_SIZE)
    blocked_decay = jnp.transpose(decay_logarithm.reshape(PAIRED_KV_PARTS, block_number, block_length), (1, 0, 2))
    position = jnp.arange(block_length)
    causal = position[:, None] >= position[None, :]

    def linear_block(state, inputs):
        query_bfloat, key_bfloat, value_bfloat, decay_b = inputs
        cum_decay = jnp.cumsum(decay_b, axis=1)
        end_decay = cum_decay[:, -1]
        gap_decay = cum_decay[:, :, None] - cum_decay[:, None, :]
        weight_mask = jnp.where(causal[None], jnp.exp(jnp.where(causal[None], gap_decay, 0.0)), 0.0)
        inner_scores = jnp.einsum('thgd,shd->hgts', query_bfloat, key_bfloat, precision=hi_prec) * weight_mask[:, None]
        inner_out = jnp.einsum('hgts,shd->thgd', inner_scores, value_bfloat, precision=hi_prec)
        carried = jnp.einsum('thgd,hde->thge', query_bfloat, state, precision=hi_prec) * jnp.exp(cum_decay).T[:, :, None, None]
        tail_weight = jnp.exp(end_decay[:, None] - cum_decay)
        local_state = jnp.einsum('shd,she->hde', key_bfloat * tail_weight.T[:, :, None], value_bfloat, precision=hi_prec)
        new_state = jnp.exp(end_decay)[:, None, None] * state + local_state
        return (new_state, inner_out + carried)
    initial_state = jnp.zeros((PAIRED_KV_PARTS, HEAD_SIZE, HEAD_SIZE), jnp.float32)
    unused_state, linear_out = lax.scan(linear_block, initial_state, (query_single, key_single, value_single, blocked_decay))
    linear_heads = linear_out.reshape(SEGMENT_ITEMS, QUERY_HEADS, HEAD_SIZE)
    mean_square = lax.optimization_barrier(jnp.mean(linear_heads * linear_heads, axis=2, keepdims=True))
    normed = (linear_heads / jnp.sqrt(mean_square + 1e-06)).reshape(SEGMENT_ITEMS, MODEL_SPAN) * lin_gain
    keys_padded = jnp.concatenate([jnp.zeros((WINDOW_KEYS, PAIRED_KV_PARTS * HEAD_SIZE), jnp.bfloat16), key_tensor], axis=0)
    values_padded = jnp.concatenate([jnp.zeros((WINDOW_KEYS, PAIRED_KV_PARTS * HEAD_SIZE), jnp.bfloat16), value_tensor], axis=0)

    def window_block(begin_offset):
        query_bfloat = lax.dynamic_slice_in_dim(queries, begin_offset, block_length, 0).astype(jnp.float32).reshape(block_length, PAIRED_KV_PARTS, group_extent, HEAD_SIZE)
        key_bfloat = lax.dynamic_slice_in_dim(keys_padded, begin_offset, block_length + WINDOW_KEYS, 0).astype(jnp.float32).reshape(block_length + WINDOW_KEYS, PAIRED_KV_PARTS, HEAD_SIZE)
        value_bfloat = lax.dynamic_slice_in_dim(values_padded, begin_offset, block_length + WINDOW_KEYS, 0).astype(jnp.float32).reshape(block_length + WINDOW_KEYS, PAIRED_KV_PARTS, HEAD_SIZE)
        raw_scores = jnp.einsum('thgd,shd->hgts', query_bfloat, key_bfloat) * scale_multiplier
        key_pos = begin_offset - WINDOW_KEYS + jnp.arange(block_length + WINDOW_KEYS, dtype=jnp.int32)
        query_pos = begin_offset + jnp.arange(block_length, dtype=jnp.int32)
        distance = query_pos[:, None] - key_pos[None, :]
        allowed = (distance >= 0) & (distance < WINDOW_KEYS) & (key_pos[None, :] >= 0)
        masked = jnp.where(allowed[None, None], raw_scores, -jnp.inf)
        row_max = lax.optimization_barrier(jnp.max(masked, axis=3, keepdims=True))
        expo_scores = jnp.exp(masked - row_max)
        probs = (expo_scores / lax.optimization_barrier(jnp.sum(expo_scores, axis=3, keepdims=True))).astype(jnp.bfloat16)
        window_out = jnp.einsum('hgts,shd->thgd', probs.astype(jnp.float32), value_bfloat)
        return window_out.reshape(block_length, MODEL_SPAN)
    starts = (jnp.arange(block_number) * block_length).astype(jnp.int32)
    window = lax.map(window_block, starts).reshape(SEGMENT_ITEMS, MODEL_SPAN)
    attn = (normed + window).astype(jnp.bfloat16)
    capacity = MOST * N_WIDE * N_NARROW
    block_units = FF // QUART
    flat_routes = routes.reshape(-1)
    gate_padded = jnp.concatenate([route_weight.reshape(-1), jnp.zeros((1,), jnp.float32)])
    attn_padded = jnp.concatenate([attn, jnp.zeros((1, MODEL_SPAN), jnp.bfloat16)], axis=0)

    def expert_step(total, expert):
        index_list = jnp.nonzero(flat_routes == expert, size=capacity, fill_value=SEGMENT_ITEMS * TOP)[0].astype(jnp.int32)
        token_ids = (index_list // TOP).astype(jnp.int32)
        token_rows = attn_padded[token_ids]
        gates = gate_padded[index_list]
        up_cols = lax.dynamic_slice_in_dim(w_up, (expert * FF).astype(jnp.int32), FF, 1)
        down_rows = lax.dynamic_slice_in_dim(w_down, (expert * FF).astype(jnp.int32), FF, 0)
        hidden = jax.nn.silu(jnp.dot(token_rows, up_cols, preferred_element_type=jnp.float32)).astype(jnp.bfloat16)
        summed = jnp.zeros((capacity, MODEL_SPAN), jnp.float32)
        for block_no in range(QUART):
            piece = jnp.dot(hidden[:, block_no * block_units:(block_no + 1) * block_units], down_rows[block_no * block_units:(block_no + 1) * block_units], preferred_element_type=jnp.float32)
            piece = lax.optimization_barrier(piece.astype(jnp.bfloat16))
            summed = summed + piece.astype(jnp.float32)
        return (total.at[token_ids].add(gates[:, None] * summed), None)
    moe_total, unused_out = lax.scan(expert_step, jnp.zeros((SEGMENT_ITEMS + 1, MODEL_SPAN), jnp.float32), jnp.arange(EXPERTS, dtype=jnp.int32))
    moe = moe_total[:SEGMENT_ITEMS]
    return (attn.astype(jnp.float32) + moe).astype(jnp.bfloat16)
```

```python
import jax
import jax.numpy as jnp
from jax import lax
from jax.experimental import pallas as pl
from jax.experimental.pallas import tpu as pltpu
from jax.sharding import PartitionSpec as P


EXPERTS = 32
QUART = 4
MOST = 12
TOK = 128
HEADS = 16
HEAD = 128
KV = 2
GROUP = HEADS // KV
WIDTH = HEADS * HEAD
UNITS = 352
PADDED = 768
PIECE = 176
PITCH = 17
CHUNK = 96
SLOTS = EXPERTS * MOST
SCALE = HEAD ** (-0.5)
BOTH = ("wide", "narrow")
F32 = jnp.float32
BF16 = jnp.bfloat16
GROUPED = True


def dot(a, b, lhs=1, rhs=0):
    return lax.dot_general(a, b, (((lhs,), (rhs,)), ((), ())), preferred_element_type=F32)


def iota(shape, dim):
    return lax.broadcasted_iota(jnp.int32, shape, dim)


def split(x):
    high = x.astype(BF16)
    return high, (x - high.astype(F32)).astype(BF16)


def decay_sums(decay_ref, head):
    total = jnp.broadcast_to(decay_ref[head : head + 1, :], (8, TOK))
    lane = iota((8, TOK), 1)
    for by in (1, 2, 4, 8, 16, 32, 64):
        total = total + jnp.where(lane >= by, pltpu.roll(total, by, 1), 0.0)
    row = jnp.broadcast_to(total[0:1, :], (TOK, TOK))
    same = iota((TOK, TOK), 0) == iota((TOK, TOK), 1)
    column = jnp.sum(jnp.where(same, row, 0.0), axis=1, keepdims=True)
    return row, column


def state_kernel(key_ref, value_ref, decay_ref, message_ref, pair_ref):
    lane = iota((HEAD, HEAD), 1)
    for head in range(KV):
        cols = slice(head * HEAD, (head + 1) * HEAD)
        row, column = decay_sums(decay_ref, head)
        last = row[:, TOK - 1 : TOK]
        weighted = key_ref[:, cols].astype(F32) * jnp.exp(last - column)
        high, low = split(weighted)
        values = value_ref[:, cols]
        state = dot(
            jnp.concatenate([high, low], axis=0), jnp.concatenate([values, values], axis=0), 0, 0
        )
        fade = jnp.exp(jnp.broadcast_to(last, (HEAD, HEAD)))
        message_ref[head * HEAD : (head + 1) * HEAD, :] = jnp.where(lane < 64, state, fade)
        message_ref[256 + head * HEAD : 256 + (head + 1) * HEAD, :] = jnp.where(
            lane < 64, pltpu.roll(state, 64, 1), fade
        )
    pair_ref[:TOK, :] = key_ref[...]
    pair_ref[TOK:, :] = value_ref[...]


def prefix_kernel(message_ref, before_ref):
    count = message_ref.shape[0]
    shape = (count, 128)
    first = iota(shape, 1) < 64
    place = iota(shape, 0)
    neutral = jnp.where(first, 0.0, 1.0)
    run = message_ref[...]
    by = 1
    while by < count:
        earlier = jnp.where(place >= by, pltpu.roll(run, by, 0), neutral)
        fade = jnp.where(first, pltpu.roll(run, 64, 1), run)
        run = earlier * fade + jnp.where(first, run, 0.0)
        by *= 2
    before_ref[...] = jnp.where(place >= 1, pltpu.roll(run, 1, 0), 0.0)


def local_kernel(
    started_ref, query_ref, key_ref, value_ref, prev_ref, decay_ref, window_ref, inner_ref
):
    seen = iota((TOK, TOK), 1) <= iota((TOK, TOK), 0)
    usable = jnp.logical_or(seen, jnp.broadcast_to(started_ref[0] > 0, (TOK, TOK)))
    for head in range(KV):
        cols = slice(head * HEAD, (head + 1) * HEAD)
        row, column = decay_sums(decay_ref, head)
        weight = jnp.where(seen, jnp.exp(jnp.where(seen, column - row, 0.0)), 0.0)
        keys = jnp.concatenate([key_ref[:, cols], prev_ref[:TOK, cols]], axis=0)
        own = value_ref[:, cols]
        values = jnp.concatenate([own, prev_ref[TOK:, cols]], axis=0)
        twice = jnp.concatenate([own, own], axis=0)

        def one(j, carry):
            here = pl.ds(pl.multiple_of((head * GROUP + j) * HEAD, HEAD), HEAD)
            scores = dot(query_ref[:, here], keys, 1, 1)
            now, prev = scores[:, :TOK], scores[:, TOK:]
            high, low = split(now * weight)
            inner_ref[:, here] = dot(jnp.concatenate([high, low], axis=1), twice)
            masked = jnp.where(usable, jnp.where(seen, now, prev) * SCALE, -jnp.inf)
            expo = jnp.exp(masked - jnp.max(masked, axis=1, keepdims=True))
            probs = expo / jnp.sum(expo, axis=1, keepdims=True)
            both = jnp.concatenate(
                [jnp.where(seen, probs, 0.0), jnp.where(seen, 0.0, probs)], axis=1
            )
            window_ref[:, here] = dot(both.astype(BF16), values)
            return carry

        lax.fori_loop(0, GROUP, one, 0, unroll=2)


def finish_kernel(
    slot_ref, query_ref, before_ref, decay_ref, gain_ref, window_ref, inner_ref, attn_ref, send_ref, rows_ref
):
    lane = iota((HEAD, HEAD), 1)
    send_ref[...] = jnp.zeros(send_ref.shape, BF16)
    for head in range(KV):
        _, column = decay_sums(decay_ref, head)
        left = before_ref[head * HEAD : (head + 1) * HEAD, :]
        right = before_ref[256 + head * HEAD : 256 + (head + 1) * HEAD, :]
        state = jnp.where(lane < 64, left, pltpu.roll(right, 64, 1))
        halves = jnp.concatenate(split(state), axis=1)
        fade = jnp.exp(column)

        def one(j, carry):
            number = head * GROUP + j
            here = pl.ds(pl.multiple_of(number * HEAD, HEAD), HEAD)
            product = dot(query_ref[:, here], halves)
            carried = (product[:, :HEAD] + product[:, HEAD:]) * fade
            linear = (carried + inner_ref[:, here]) * SCALE
            mean = jnp.mean(linear * linear, axis=1, keepdims=True)
            normed = linear / jnp.sqrt(mean + 1e-06) * gain_ref[:, here]
            rows_ref[pl.ds(number, TOK, stride=PITCH), :] = normed + window_ref[:, here]
            return carry

        lax.fori_loop(0, GROUP, one, 0, unroll=2)

    def place(t, carry):
        row = rows_ref[pl.ds(t * PITCH, HEADS), :].astype(BF16)
        attn_ref[t] = row
        send_ref[slot_ref[2 * t]] = row
        send_ref[slot_ref[2 * t + 1]] = row
        return carry

    lax.fori_loop(0, TOK, place, 0, unroll=8)


def pick_kernel(plane_ref, up_ref, down_ref, piece_ref, sem):
    plane = plane_ref[0]
    rows = pl.ds(pl.multiple_of(lax.rem(plane, 2) * PIECE, PIECE), PIECE)

    @pl.when(plane < 2)
    def from_up():
        pltpu.make_async_copy(up_ref.at[rows, :], piece_ref, sem).start()

    @pl.when(plane >= 2)
    def from_down():
        pltpu.make_async_copy(down_ref.at[rows, :], piece_ref, sem).start()

    pltpu.make_async_copy(down_ref.at[rows, :], piece_ref, sem).wait()


def expert_kernel(plane_ref, recv_ref, *refs):
    sources, rest = refs[:12], refs[12:]
    out_ref, tiles_ref, rows_ref, x_ref, held_ref, hidden_ref, sems, tile_sems = rest
    plane = plane_ref[0]
    up_ref = held_ref.at[pl.ds(0, QUART * UNITS), :]
    down_ref = held_ref.at[pl.ds(QUART * UNITS, 2 * PADDED), :]
    down_at = QUART * UNITS
    arrivals = []
    for n in range(SLOTS // CHUNK):
        some = pl.ds(n * CHUNK, CHUNK)
        arrivals.append(
            pltpu.make_async_copy(recv_ref.at[some], tiles_ref.at[some], tile_sems.at[n])
        )
        arrivals[n].start()
    copies = []
    for n, at in enumerate((0, down_at, UNITS, down_at + UNITS)):
        copies.append(
            pltpu.make_async_copy(sources[n], held_ref.at[pl.ds(at, UNITS), :], sems.at[n])
        )
    for n in range(8):
        shard, step = n // 4, n % 4
        quarter = lax.rem(plane - step + 4, 4)
        at = jnp.where(
            quarter < 2,
            (2 + shard) * UNITS + quarter * PIECE,
            down_at + PADDED + shard * UNITS + (quarter - 2) * PIECE,
        )
        place = pl.ds(pl.multiple_of(at, PIECE // 11), PIECE)
        copies.append(
            pltpu.make_async_copy(sources[4 + n], held_ref.at[place, :], sems.at[4 + n])
        )
    for n in (0, 2, 1, 3, 4, 5, 6, 7, 8, 9, 10, 11):
        copies[n].start()
    for half in range(2):
        end = (half + 1) * PADDED
        down_ref[end - 64 : end, :] = jnp.zeros((64, WIDTH), BF16)
        hidden_ref[:, end - 128 : end] = jnp.zeros((SLOTS, 128), BF16)

    def unpack(t, carry):
        rows_ref[pl.ds(t * PITCH, HEADS), :] = tiles_ref[t].astype(F32)
        return carry

    for n in range(SLOTS // CHUNK):
        arrivals[n].wait()
        lax.fori_loop(n * CHUNK, (n + 1) * CHUNK, unpack, 0, unroll=16)
    for j in range(HEADS):
        x_ref[:, j * HEAD : (j + 1) * HEAD] = rows_ref[
            pl.ds(j, SLOTS, stride=PITCH), :
        ].astype(BF16)
    for half in range(2):
        for n in ((0, 2), (1, 3, 4, 5, 6, 7, 8, 9, 10, 11))[half]:
            copies[n].wait()
        for start, size in ((0, 256), (256, 256), (512, 192)):
            at = half * 2 * UNITS + start
            hidden = 0.5 * dot(x_ref[...], up_ref[at : at + size, :], 1, 1)
            hidden = hidden + hidden * jnp.tanh(hidden)
            at = half * PADDED + start
            hidden_ref[:, at : at + size] = hidden.astype(BF16)

    def columns(n, carry):
        here = pl.ds(pl.multiple_of(n * 256, 256), 256)
        result = dot(hidden_ref[...], down_ref[:, here])
        rows_ref[pl.ds(2 * n, SLOTS, stride=PITCH), :] = result[:, :HEAD]
        rows_ref[pl.ds(2 * n + 1, SLOTS, stride=PITCH), :] = result[:, HEAD:]
        return carry

    lax.fori_loop(0, WIDTH // 256, columns, 0, unroll=4)

    def pack(t, carry):
        tiles_ref[t] = rows_ref[pl.ds(t * PITCH, HEADS), :].astype(BF16)
        return carry

    leaving = []
    for n in range(SLOTS // CHUNK):
        lax.fori_loop(n * CHUNK, (n + 1) * CHUNK, pack, 0, unroll=16)
        some = pl.ds(n * CHUNK, CHUNK)
        leaving.append(pltpu.make_async_copy(tiles_ref.at[some], out_ref.at[some], tile_sems.at[n]))
        leaving[n].start()
    for one in leaving:
        one.wait()


def combine_kernel(slot_ref, gate_ref, back_ref, attn_ref, out_ref, rows_ref):
    def one(t, carry):
        moe = back_ref[slot_ref[2 * t]].astype(F32) * gate_ref[2 * t]
        moe = moe + back_ref[slot_ref[2 * t + 1]].astype(F32) * gate_ref[2 * t + 1]
        rows_ref[pl.ds(t * PITCH, HEADS), :] = attn_ref[t].astype(F32) + moe
        return carry

    lax.fori_loop(0, TOK, one, 0, unroll=8)
    for j in range(HEADS):
        out_ref[:, j * HEAD : (j + 1) * HEAD] = rows_ref[
            pl.ds(j, TOK, stride=PITCH), :
        ].astype(BF16)


VMEM = pl.BlockSpec(memory_space=pltpu.VMEM)
SMEM = pl.BlockSpec(memory_space=pltpu.SMEM)
FAR = pl.BlockSpec(memory_space=pltpu.HBM)


def call(kernel, outs, in_specs, scratch=(), flops=0, moved=0, exps=0, room=16, place=VMEM):
    shapes = [jax.ShapeDtypeStruct(shape, dtype) for shape, dtype in outs]
    return pl.pallas_call(
        kernel,
        out_shape=shapes if len(shapes) > 1 else shapes[0],
        in_specs=in_specs,
        out_specs=[place] * len(shapes) if len(shapes) > 1 else place,
        scratch_shapes=list(scratch),
        compiler_params=pltpu.CompilerParams(vmem_limit_bytes=room << 20),
        cost_estimate=pl.CostEstimate(flops=flops, bytes_accessed=moved, transcendentals=exps),
    )


def swapped(x, bit):
    peers = lax.axis_size("wide")
    return lax.ppermute(x, "wide", [(i, i ^ bit) for i in range(peers)])


def exchanged(x, axis):
    return lax.all_to_all(x, axis, split_axis=0, concat_axis=0, tiled=True)


def routed(rows):
    flat = rows.reshape(SLOTS * HEADS, HEAD)
    groups = [[e * QUART + q for e in range(EXPERTS)] for q in range(QUART)] if GROUPED else None
    traded = lax.all_to_all(
        flat, "wide", split_axis=0, concat_axis=0, tiled=True, axis_index_groups=groups
    )
    return traded.reshape(rows.shape)


def per_device(
    queries, key_tensor, value_tensor, decay_logarithm, lin_gain, routes, route_weight, w_up, w_down
):
    devices = lax.axis_size(BOTH)
    message, pair = call(
        state_kernel,
        [((devices, 128), F32), ((2 * TOK, KV * HEAD), BF16)],
        [VMEM] * 3,
        room=58,
        flops=1 << 24,
        moved=600_000,
    )(key_tensor, value_tensor, decay_logarithm)
    gathered = exchanged(message, BOTH)
    previous = lax.ppermute(pair, BOTH, [(i, i + 1) for i in range(devices - 1)])
    up = w_up.T
    plane = lax.axis_index("narrow").astype(jnp.int32).reshape(1)
    planes = lax.axis_size("narrow")
    piece = call(
        pick_kernel,
        [((PIECE, WIDTH), BF16)],
        [SMEM, FAR, FAR],
        [pltpu.SemaphoreType.DMA],
        room=58,
        moved=1_400_000,
    )(plane, up, w_down)
    pieces = [swapped(piece, 2)]
    for by in (1, 2, 3):
        around = [(i, (i + by) % planes) for i in range(planes)]
        pieces.append(lax.ppermute(pieces[0], "narrow", around))
    up_c, down_c = swapped(up, 1), swapped(w_down, 1)
    onward = [swapped(one, 1) for one in pieces]

    before = call(
        prefix_kernel, [((devices, 128), F32)], [VMEM], flops=1 << 22, moved=524_288
    )(gathered)
    before = exchanged(before, BOTH)

    flat = routes.reshape(-1)
    onehot = (flat[:, None] == jnp.arange(EXPERTS)[None, :]).astype(jnp.int32)
    rank = jnp.sum((jnp.cumsum(onehot, axis=0) - onehot) * onehot, axis=1)
    slots = flat * MOST + rank
    started = jnp.minimum(lax.axis_index(BOTH), 1).astype(jnp.int32).reshape(1)
    window, inner = call(
        local_kernel,
        [((TOK, WIDTH), F32)] * 2,
        [SMEM] + [VMEM] * 5,
        flops=1 << 29,
        moved=3_000_000,
        exps=1 << 18,
    )(started, queries, key_tensor, value_tensor, previous, decay_logarithm)
    attn, send = call(
        finish_kernel,
        [((TOK, HEADS, HEAD), BF16), ((SLOTS, HEADS, HEAD), BF16)],
        [SMEM] + [VMEM] * 6,
        [pltpu.VMEM((TOK * PITCH, HEAD), F32)],
        flops=1 << 28,
        moved=5_000_000,
    )(slots, queries, before, decay_logarithm, lin_gain.reshape(1, WIDTH), window, inner)

    received = routed(send)
    computed = call(
        expert_kernel,
        [((SLOTS, HEADS, HEAD), BF16)],
        [SMEM] + [FAR] * 13,
        [
            pltpu.VMEM((SLOTS, HEADS, HEAD), BF16),
            pltpu.VMEM((SLOTS * PITCH, HEAD), F32),
            pltpu.VMEM((SLOTS, WIDTH), BF16),
            pltpu.VMEM((QUART * UNITS + 2 * PADDED, WIDTH), BF16),
            pltpu.VMEM((SLOTS, 2 * PADDED), BF16),
            pltpu.SemaphoreType.DMA((12,)),
            pltpu.SemaphoreType.DMA((SLOTS // CHUNK,)),
        ],
        room=62,
        place=FAR,
        flops=4_500_000_000,
        moved=15_000_000,
        exps=1 << 19,
    )(plane, received, up, w_down, up_c, down_c, *pieces, *onward)
    back = routed(computed)
    return call(
        combine_kernel,
        [((TOK, WIDTH), BF16)],
        [SMEM] * 2 + [VMEM] * 2,
        [pltpu.VMEM((TOK * PITCH, HEAD), F32)],
        flops=1 << 20,
        moved=2_600_000,
    )(slots, route_weight.reshape(-1), back, attn)


def solution(mesh):
    rows = P(("wide", "narrow"), None)
    in_specs = (rows, rows, rows, P(None, ("wide", "narrow")), P(), rows, rows, P(None, "wide"), P("wide", None))
    return jax.shard_map(per_device, mesh=mesh, in_specs=in_specs, out_specs=rows, check_vma=False)
```

```python
import jax
import jax.numpy as jnp
from jax import lax
from jax.experimental import pallas as pl
from jax.experimental.pallas import tpu as pltpu
from jax.sharding import PartitionSpec as P


EXPERTS = 32
QUART = 4
MOST = 12
TOK = 128
HEADS = 16
HEAD = 128
KV = 2
GROUP = HEADS // KV
WIDTH = HEADS * HEAD
UNITS = 352
PADDED = 1536
PIECE = 176
PITCH = 17
CHUNK = 96
SLOTS = EXPERTS * MOST
SCALE = HEAD ** (-0.5)
BOTH = ("wide", "narrow")
F32 = jnp.float32
BF16 = jnp.bfloat16
GROUPED = True


def dot(a, b, lhs=1, rhs=0):
    return lax.dot_general(a, b, (((lhs,), (rhs,)), ((), ())), preferred_element_type=F32)


def iota(shape, dim):
    return lax.broadcasted_iota(jnp.int32, shape, dim)


def split(x):
    high = x.astype(BF16)
    return high, (x - high.astype(F32)).astype(BF16)


def decay_sums(decay_ref, head):
    total = jnp.broadcast_to(decay_ref[head : head + 1, :], (8, TOK))
    lane = iota((8, TOK), 1)
    for by in (1, 2, 4, 8, 16, 32, 64):
        total = total + jnp.where(lane >= by, pltpu.roll(total, by, 1), 0.0)
    row = jnp.broadcast_to(total[0:1, :], (TOK, TOK))
    same = iota((TOK, TOK), 0) == iota((TOK, TOK), 1)
    column = jnp.sum(jnp.where(same, row, 0.0), axis=1, keepdims=True)
    return row, column


def state_kernel(key_ref, value_ref, decay_ref, message_ref, pair_ref):
    lane = iota((HEAD, HEAD), 1)
    for head in range(KV):
        cols = slice(head * HEAD, (head + 1) * HEAD)
        row, column = decay_sums(decay_ref, head)
        last = row[:, TOK - 1 : TOK]
        weighted = key_ref[:, cols].astype(F32) * jnp.exp(last - column)
        high, low = split(weighted)
        values = value_ref[:, cols]
        state = dot(
            jnp.concatenate([high, low], axis=0), jnp.concatenate([values, values], axis=0), 0, 0
        )
        fade = jnp.exp(jnp.broadcast_to(last, (HEAD, HEAD)))
        message_ref[head * HEAD : (head + 1) * HEAD, :] = jnp.where(lane < 64, state, fade)
        message_ref[256 + head * HEAD : 256 + (head + 1) * HEAD, :] = jnp.where(
            lane < 64, pltpu.roll(state, 64, 1), fade
        )
    pair_ref[:TOK, :] = key_ref[...]
    pair_ref[TOK:, :] = value_ref[...]


def prefix_kernel(message_ref, before_ref):
    count = message_ref.shape[0]
    shape = (count, 128)
    first = iota(shape, 1) < 64
    place = iota(shape, 0)
    neutral = jnp.where(first, 0.0, 1.0)
    run = message_ref[...]
    by = 1
    while by < count:
        earlier = jnp.where(place >= by, pltpu.roll(run, by, 0), neutral)
        fade = jnp.where(first, pltpu.roll(run, 64, 1), run)
        run = earlier * fade + jnp.where(first, run, 0.0)
        by *= 2
    before_ref[...] = jnp.where(place >= 1, pltpu.roll(run, 1, 0), 0.0)


def local_kernel(
    started_ref, query_ref, key_ref, value_ref, prev_ref, decay_ref, window_ref, inner_ref
):
    seen = iota((TOK, TOK), 1) <= iota((TOK, TOK), 0)
    usable = jnp.logical_or(seen, jnp.broadcast_to(started_ref[0] > 0, (TOK, TOK)))
    for head in range(KV):
        cols = slice(head * HEAD, (head + 1) * HEAD)
        row, column = decay_sums(decay_ref, head)
        weight = jnp.where(seen, jnp.exp(jnp.where(seen, column - row, 0.0)), 0.0)
        keys = jnp.concatenate([key_ref[:, cols], prev_ref[:TOK, cols]], axis=0)
        own = value_ref[:, cols]
        values = jnp.concatenate([own, prev_ref[TOK:, cols]], axis=0)
        twice = jnp.concatenate([own, own], axis=0)

        def one(j, carry):
            here = pl.ds(pl.multiple_of((head * GROUP + j) * HEAD, HEAD), HEAD)
            scores = dot(query_ref[:, here], keys, 1, 1)
            now, prev = scores[:, :TOK], scores[:, TOK:]
            high, low = split(now * weight)
            inner_ref[:, here] = dot(jnp.concatenate([high, low], axis=1), twice)
            masked = jnp.where(usable, jnp.where(seen, now, prev) * SCALE, -jnp.inf)
            expo = jnp.exp(masked - jnp.max(masked, axis=1, keepdims=True))
            probs = expo / jnp.sum(expo, axis=1, keepdims=True)
            both = jnp.concatenate(
                [jnp.where(seen, probs, 0.0), jnp.where(seen, 0.0, probs)], axis=1
            )
            window_ref[:, here] = dot(both.astype(BF16), values)
            return carry

        lax.fori_loop(0, GROUP, one, 0, unroll=2)


def finish_kernel(
    slot_ref, query_ref, before_ref, decay_ref, gain_ref, window_ref, inner_ref, attn_ref, send_ref, rows_ref
):
    lane = iota((HEAD, HEAD), 1)
    send_ref[...] = jnp.zeros(send_ref.shape, BF16)
    for head in range(KV):
        _, column = decay_sums(decay_ref, head)
        left = before_ref[head * HEAD : (head + 1) * HEAD, :]
        right = before_ref[256 + head * HEAD : 256 + (head + 1) * HEAD, :]
        state = jnp.where(lane < 64, left, pltpu.roll(right, 64, 1))
        halves = jnp.concatenate(split(state), axis=1)
        fade = jnp.exp(column)

        def one(j, carry):
            number = head * GROUP + j
            here = pl.ds(pl.multiple_of(number * HEAD, HEAD), HEAD)
            product = dot(query_ref[:, here], halves)
            carried = (product[:, :HEAD] + product[:, HEAD:]) * fade
            linear = (carried + inner_ref[:, here]) * SCALE
            mean = jnp.mean(linear * linear, axis=1, keepdims=True)
            normed = linear / jnp.sqrt(mean + 1e-06) * gain_ref[:, here]
            rows_ref[pl.ds(number, TOK, stride=PITCH), :] = normed + window_ref[:, here]
            return carry

        lax.fori_loop(0, GROUP, one, 0, unroll=2)

    def place(t, carry):
        row = rows_ref[pl.ds(t * PITCH, HEADS), :].astype(BF16)
        attn_ref[t] = row
        send_ref[slot_ref[2 * t]] = row
        send_ref[slot_ref[2 * t + 1]] = row
        return carry

    lax.fori_loop(0, TOK, place, 0, unroll=8)


def pick_kernel(plane_ref, up_ref, down_ref, piece_ref, sem):
    plane = plane_ref[0]
    rows = pl.ds(pl.multiple_of(lax.rem(plane, 2) * PIECE, PIECE), PIECE)

    @pl.when(plane < 2)
    def from_up():
        pltpu.make_async_copy(up_ref.at[rows, :], piece_ref, sem).start()

    @pl.when(plane >= 2)
    def from_down():
        pltpu.make_async_copy(down_ref.at[rows, :], piece_ref, sem).start()

    pltpu.make_async_copy(down_ref.at[rows, :], piece_ref, sem).wait()


def assemble_kernel(plane_ref, *refs):
    sources, (held_ref, sems) = refs[:12], refs[12:]
    plane = plane_ref[0]
    copies = []
    for n, at in enumerate((0, PADDED, UNITS, PADDED + UNITS)):
        copies.append(
            pltpu.make_async_copy(sources[n], held_ref.at[pl.ds(at, UNITS), :], sems.at[n])
        )
    for n in range(8):
        shard, step = n // 4, n % 4
        quarter = lax.rem(plane - step + 4, 4)
        at = (2 + shard) * UNITS + lax.rem(quarter, 2) * PIECE
        at = at + jnp.where(quarter < 2, 0, PADDED)
        place = pl.ds(pl.multiple_of(at, PIECE // 11), PIECE)
        copies.append(
            pltpu.make_async_copy(sources[4 + n], held_ref.at[place, :], sems.at[4 + n])
        )
    for one in copies:
        one.start()
    empty = jnp.zeros((PADDED - QUART * UNITS, WIDTH), BF16)
    for end in (PADDED, 2 * PADDED):
        held_ref[end - PADDED + QUART * UNITS : end, :] = empty
    for one in copies:
        one.wait()


def expert_kernel(
    recv_ref, weight_ref, out_ref, tiles_ref, rows_ref, x_ref, held_ref, hidden_ref, sems, weight_sems
):
    arrivals = []
    for n in range(SLOTS // CHUNK):
        some = pl.ds(n * CHUNK, CHUNK)
        arrivals.append(pltpu.make_async_copy(recv_ref.at[some], tiles_ref.at[some], sems.at[n]))
    parts = []
    for n, (at, size) in enumerate(((0, 512), (512, 1024), (1536, 1536))):
        some = pl.ds(at, size)
        parts.append(
            pltpu.make_async_copy(weight_ref.at[some, :], held_ref.at[some, :], weight_sems.at[n])
        )
    for one in arrivals + parts:
        one.start()

    def unpack(t, carry):
        rows_ref[pl.ds(t * PITCH, HEADS), :] = tiles_ref[t].astype(F32)
        return carry

    for n in range(SLOTS // CHUNK):
        arrivals[n].wait()
        lax.fori_loop(n * CHUNK, (n + 1) * CHUNK, unpack, 0, unroll=16)
    for j in range(HEADS):
        x_ref[:, j * HEAD : (j + 1) * HEAD] = rows_ref[
            pl.ds(j, SLOTS, stride=PITCH), :
        ].astype(BF16)
    for part, blocks in ((0, (0, 1)), (1, (2, 3, 4, 5))):
        parts[part].wait()
        for n in blocks:
            here = slice(n * 256, (n + 1) * 256)
            hidden = 0.5 * dot(x_ref[...], held_ref[here, :], 1, 1)
            hidden_ref[:, here] = (hidden + hidden * jnp.tanh(hidden)).astype(BF16)
    parts[2].wait()

    def columns(n, carry):
        here = pl.ds(pl.multiple_of(n * 256, 256), 256)
        result = dot(hidden_ref[...], held_ref[PADDED:, here])
        rows_ref[pl.ds(2 * n, SLOTS, stride=PITCH), :] = result[:, :HEAD]
        rows_ref[pl.ds(2 * n + 1, SLOTS, stride=PITCH), :] = result[:, HEAD:]
        return carry

    lax.fori_loop(0, WIDTH // 256, columns, 0, unroll=4)

    def pack(t, carry):
        tiles_ref[t] = rows_ref[pl.ds(t * PITCH, HEADS), :].astype(BF16)
        return carry

    leaving = []
    for n in range(SLOTS // CHUNK):
        lax.fori_loop(n * CHUNK, (n + 1) * CHUNK, pack, 0, unroll=16)
        some = pl.ds(n * CHUNK, CHUNK)
        leaving.append(pltpu.make_async_copy(tiles_ref.at[some], out_ref.at[some], sems.at[n]))
        leaving[n].start()
    for one in leaving:
        one.wait()


def combine_kernel(slot_ref, gate_ref, back_ref, attn_ref, out_ref, rows_ref):
    def one(t, carry):
        moe = back_ref[slot_ref[2 * t]].astype(F32) * gate_ref[2 * t]
        moe = moe + back_ref[slot_ref[2 * t + 1]].astype(F32) * gate_ref[2 * t + 1]
        rows_ref[pl.ds(t * PITCH, HEADS), :] = attn_ref[t].astype(F32) + moe
        return carry

    lax.fori_loop(0, TOK, one, 0, unroll=8)
    for j in range(HEADS):
        out_ref[:, j * HEAD : (j + 1) * HEAD] = rows_ref[
            pl.ds(j, TOK, stride=PITCH), :
        ].astype(BF16)


VMEM = pl.BlockSpec(memory_space=pltpu.VMEM)
SMEM = pl.BlockSpec(memory_space=pltpu.SMEM)
FAR = pl.BlockSpec(memory_space=pltpu.HBM)


def call(kernel, outs, in_specs, scratch=(), flops=0, moved=0, exps=0, room=16, place=VMEM):
    shapes = [jax.ShapeDtypeStruct(shape, dtype) for shape, dtype in outs]
    return pl.pallas_call(
        kernel,
        out_shape=shapes if len(shapes) > 1 else shapes[0],
        in_specs=in_specs,
        out_specs=[place] * len(shapes) if len(shapes) > 1 else place,
        scratch_shapes=list(scratch),
        compiler_params=pltpu.CompilerParams(vmem_limit_bytes=room << 20),
        cost_estimate=pl.CostEstimate(flops=flops, bytes_accessed=moved, transcendentals=exps),
    )


def swapped(x, bit):
    peers = lax.axis_size("wide")
    return lax.ppermute(x, "wide", [(i, i ^ bit) for i in range(peers)])


def exchanged(x, axis):
    return lax.all_to_all(x, axis, split_axis=0, concat_axis=0, tiled=True)


def routed(rows):
    flat = rows.reshape(SLOTS * HEADS, HEAD)
    groups = [[e * QUART + q for e in range(EXPERTS)] for q in range(QUART)] if GROUPED else None
    traded = lax.all_to_all(
        flat, "wide", split_axis=0, concat_axis=0, tiled=True, axis_index_groups=groups
    )
    return traded.reshape(rows.shape)


def per_device(
    queries, key_tensor, value_tensor, decay_logarithm, lin_gain, routes, route_weight, w_up, w_down
):
    devices = lax.axis_size(BOTH)
    message, pair = call(
        state_kernel,
        [((devices, 128), F32), ((2 * TOK, KV * HEAD), BF16)],
        [VMEM] * 3,
        room=58,
        flops=1 << 24,
        moved=600_000,
    )(key_tensor, value_tensor, decay_logarithm)
    gathered = exchanged(message, BOTH)
    previous = lax.ppermute(pair, BOTH, [(i, i + 1) for i in range(devices - 1)])
    up = w_up.T
    plane = lax.axis_index("narrow").astype(jnp.int32).reshape(1)
    planes = lax.axis_size("narrow")
    piece = call(
        pick_kernel,
        [((PIECE, WIDTH), BF16)],
        [SMEM, FAR, FAR],
        [pltpu.SemaphoreType.DMA],
        room=58,
        moved=1_400_000,
    )(plane, up, w_down)
    pieces = [swapped(piece, 2)]
    for by in (1, 2, 3):
        around = [(i, (i + by) % planes) for i in range(planes)]
        pieces.append(lax.ppermute(pieces[0], "narrow", around))
    up_c, down_c = swapped(up, 1), swapped(w_down, 1)
    onward = [swapped(one, 1) for one in pieces]

    before = call(
        prefix_kernel, [((devices, 128), F32)], [VMEM], flops=1 << 22, moved=524_288
    )(gathered)
    before = exchanged(before, BOTH)

    flat = routes.reshape(-1)
    onehot = (flat[:, None] == jnp.arange(EXPERTS)[None, :]).astype(jnp.int32)
    rank = jnp.sum((jnp.cumsum(onehot, axis=0) - onehot) * onehot, axis=1)
    slots = flat * MOST + rank
    started = jnp.minimum(lax.axis_index(BOTH), 1).astype(jnp.int32).reshape(1)
    window, inner = call(
        local_kernel,
        [((TOK, WIDTH), F32)] * 2,
        [SMEM] + [VMEM] * 5,
        flops=1 << 29,
        moved=3_000_000,
        exps=1 << 18,
    )(started, queries, key_tensor, value_tensor, previous, decay_logarithm)
    attn, send = call(
        finish_kernel,
        [((TOK, HEADS, HEAD), BF16), ((SLOTS, HEADS, HEAD), BF16)],
        [SMEM] + [VMEM] * 6,
        [pltpu.VMEM((TOK * PITCH, HEAD), F32)],
        flops=1 << 28,
        moved=5_000_000,
    )(slots, queries, before, decay_logarithm, lin_gain.reshape(1, WIDTH), window, inner)

    received = routed(send)
    held = call(
        assemble_kernel,
        [((2 * PADDED, WIDTH), BF16)],
        [SMEM] + [FAR] * 12,
        [pltpu.SemaphoreType.DMA((12,))],
        room=62,
        moved=24_000_000,
    )(plane, up, w_down, up_c, down_c, *pieces, *onward)
    computed = call(
        expert_kernel,
        [((SLOTS, HEADS, HEAD), BF16)],
        [FAR] * 2,
        [
            pltpu.VMEM((SLOTS, HEADS, HEAD), BF16),
            pltpu.VMEM((SLOTS * PITCH, HEAD), F32),
            pltpu.VMEM((SLOTS, WIDTH), BF16),
            pltpu.VMEM((2 * PADDED, WIDTH), BF16),
            pltpu.VMEM((SLOTS, PADDED), BF16),
            pltpu.SemaphoreType.DMA((SLOTS // CHUNK,)),
            pltpu.SemaphoreType.DMA((3,)),
        ],
        room=62,
        place=FAR,
        flops=4_500_000_000,
        moved=15_000_000,
        exps=1 << 19,
    )(received, held)
    back = routed(computed)
    return call(
        combine_kernel,
        [((TOK, WIDTH), BF16)],
        [SMEM] * 2 + [VMEM] * 2,
        [pltpu.VMEM((TOK * PITCH, HEAD), F32)],
        flops=1 << 20,
        moved=2_600_000,
    )(slots, route_weight.reshape(-1), back, attn)


def solution(mesh):
    rows = P(("wide", "narrow"), None)
    in_specs = (rows, rows, rows, P(None, ("wide", "narrow")), P(), rows, rows, P(None, "wide"), P("wide", None))
    return jax.shard_map(per_device, mesh=mesh, in_specs=in_specs, out_specs=rows, check_vma=False)
```

```python
import jax
import jax.numpy as jnp
from jax import lax
from jax.experimental import pallas as pl
from jax.experimental.pallas import tpu as pltpu
from jax.sharding import PartitionSpec as P


EXPERTS = 32
QUART = 4
MOST = 12
TOK = 128
HEADS = 16
HEAD = 128
KV = 2
GROUP = HEADS // KV
WIDTH = HEADS * HEAD
UNITS = 352
PADDED = 1536
PIECE = 176
PITCH = 17
CHUNK = 96
SLOTS = EXPERTS * MOST
SCALE = HEAD ** (-0.5)
BOTH = ("wide", "narrow")
F32 = jnp.float32
BF16 = jnp.bfloat16
GROUPED = True


def dot(a, b, lhs=1, rhs=0):
    return lax.dot_general(a, b, (((lhs,), (rhs,)), ((), ())), preferred_element_type=F32)


def iota(shape, dim):
    return lax.broadcasted_iota(jnp.int32, shape, dim)


def split(x):
    high = x.astype(BF16)
    return high, (x - high.astype(F32)).astype(BF16)


def decay_sums(decay_ref, head):
    total = jnp.broadcast_to(decay_ref[head : head + 1, :], (8, TOK))
    lane = iota((8, TOK), 1)
    for by in (1, 2, 4, 8, 16, 32, 64):
        total = total + jnp.where(lane >= by, pltpu.roll(total, by, 1), 0.0)
    row = jnp.broadcast_to(total[0:1, :], (TOK, TOK))
    same = iota((TOK, TOK), 0) == iota((TOK, TOK), 1)
    column = jnp.sum(jnp.where(same, row, 0.0), axis=1, keepdims=True)
    return row, column


def state_kernel(key_ref, value_ref, decay_ref, message_ref, pair_ref):
    lane = iota((HEAD, HEAD), 1)
    for head in range(KV):
        cols = slice(head * HEAD, (head + 1) * HEAD)
        row, column = decay_sums(decay_ref, head)
        last = row[:, TOK - 1 : TOK]
        weighted = key_ref[:, cols].astype(F32) * jnp.exp(last - column)
        high, low = split(weighted)
        values = value_ref[:, cols]
        state = dot(
            jnp.concatenate([high, low], axis=0), jnp.concatenate([values, values], axis=0), 0, 0
        )
        fade = jnp.exp(jnp.broadcast_to(last, (HEAD, HEAD)))
        message_ref[head * HEAD : (head + 1) * HEAD, :] = jnp.where(lane < 64, state, fade)
        message_ref[256 + head * HEAD : 256 + (head + 1) * HEAD, :] = jnp.where(
            lane < 64, pltpu.roll(state, 64, 1), fade
        )
    pair_ref[:TOK, :] = key_ref[...]
    pair_ref[TOK:, :] = value_ref[...]


def prefix_kernel(message_ref, before_ref):
    count = message_ref.shape[0]
    shape = (count, 128)
    first = iota(shape, 1) < 64
    place = iota(shape, 0)
    neutral = jnp.where(first, 0.0, 1.0)
    run = message_ref[...]
    by = 1
    while by < count:
        earlier = jnp.where(place >= by, pltpu.roll(run, by, 0), neutral)
        fade = jnp.where(first, pltpu.roll(run, 64, 1), run)
        run = earlier * fade + jnp.where(first, run, 0.0)
        by *= 2
    before_ref[...] = jnp.where(place >= 1, pltpu.roll(run, 1, 0), 0.0)


def local_kernel(
    started_ref, query_ref, key_ref, value_ref, prev_ref, decay_ref, window_ref, inner_ref
):
    seen = iota((TOK, TOK), 1) <= iota((TOK, TOK), 0)
    usable = jnp.logical_or(seen, jnp.broadcast_to(started_ref[0] > 0, (TOK, TOK)))
    for head in range(KV):
        cols = slice(head * HEAD, (head + 1) * HEAD)
        row, column = decay_sums(decay_ref, head)
        weight = jnp.where(seen, jnp.exp(jnp.where(seen, column - row, 0.0)), 0.0)
        keys = jnp.concatenate([key_ref[:, cols], prev_ref[:TOK, cols]], axis=0)
        own = value_ref[:, cols]
        values = jnp.concatenate([own, prev_ref[TOK:, cols]], axis=0)
        twice = jnp.concatenate([own, own], axis=0)

        def one(j, carry):
            here = pl.ds(pl.multiple_of((head * GROUP + j) * HEAD, HEAD), HEAD)
            scores = dot(query_ref[:, here], keys, 1, 1)
            now, prev = scores[:, :TOK], scores[:, TOK:]
            high, low = split(now * weight)
            inner_ref[:, here] = dot(jnp.concatenate([high, low], axis=1), twice)
            masked = jnp.where(usable, jnp.where(seen, now, prev) * SCALE, -jnp.inf)
            expo = jnp.exp(masked - jnp.max(masked, axis=1, keepdims=True))
            probs = expo / jnp.sum(expo, axis=1, keepdims=True)
            both = jnp.concatenate(
                [jnp.where(seen, probs, 0.0), jnp.where(seen, 0.0, probs)], axis=1
            )
            window_ref[:, here] = dot(both.astype(BF16), values)
            return carry

        lax.fori_loop(0, GROUP, one, 0, unroll=8)


def finish_kernel(
    slot_ref, query_ref, before_ref, decay_ref, gain_ref, window_ref, inner_ref, attn_ref, send_ref, rows_ref
):
    lane = iota((HEAD, HEAD), 1)
    send_ref[...] = jnp.zeros(send_ref.shape, BF16)
    for head in range(KV):
        _, column = decay_sums(decay_ref, head)
        left = before_ref[head * HEAD : (head + 1) * HEAD, :]
        right = before_ref[256 + head * HEAD : 256 + (head + 1) * HEAD, :]
        state = jnp.where(lane < 64, left, pltpu.roll(right, 64, 1))
        halves = jnp.concatenate(split(state), axis=1)
        fade = jnp.exp(column)

        def one(j, carry):
            number = head * GROUP + j
            here = pl.ds(pl.multiple_of(number * HEAD, HEAD), HEAD)
            product = dot(query_ref[:, here], halves)
            carried = (product[:, :HEAD] + product[:, HEAD:]) * fade
            linear = (carried + inner_ref[:, here]) * SCALE
            mean = jnp.mean(linear * linear, axis=1, keepdims=True)
            normed = linear / jnp.sqrt(mean + 1e-06) * gain_ref[:, here]
            rows_ref[pl.ds(number, TOK, stride=PITCH), :] = normed + window_ref[:, here]
            return carry

        lax.fori_loop(0, GROUP, one, 0, unroll=8)

    def place(t, carry):
        row = rows_ref[pl.ds(t * PITCH, HEADS), :].astype(BF16)
        attn_ref[t] = row
        send_ref[slot_ref[2 * t]] = row
        send_ref[slot_ref[2 * t + 1]] = row
        return carry

    lax.fori_loop(0, TOK, place, 0, unroll=16)


def pick_kernel(plane_ref, up_ref, down_ref, piece_ref, sem):
    plane = plane_ref[0]
    rows = pl.ds(pl.multiple_of(lax.rem(plane, 2) * PIECE, PIECE), PIECE)

    @pl.when(plane < 2)
    def from_up():
        pltpu.make_async_copy(up_ref.at[rows, :], piece_ref, sem).start()

    @pl.when(plane >= 2)
    def from_down():
        pltpu.make_async_copy(down_ref.at[rows, :], piece_ref, sem).start()

    pltpu.make_async_copy(down_ref.at[rows, :], piece_ref, sem).wait()


def assemble_kernel(plane_ref, *refs):
    sources, (held_ref, sems) = refs[:12], refs[12:]
    plane = plane_ref[0]
    copies = []
    for n, at in enumerate((0, PADDED, UNITS, PADDED + UNITS)):
        copies.append(
            pltpu.make_async_copy(sources[n], held_ref.at[pl.ds(at, UNITS), :], sems.at[n])
        )
    for n in range(8):
        shard, step = n // 4, n % 4
        quarter = lax.rem(plane - step + 4, 4)
        at = (2 + shard) * UNITS + lax.rem(quarter, 2) * PIECE
        at = at + jnp.where(quarter < 2, 0, PADDED)
        place = pl.ds(pl.multiple_of(at, PIECE // 11), PIECE)
        copies.append(
            pltpu.make_async_copy(sources[4 + n], held_ref.at[place, :], sems.at[4 + n])
        )
    for one in copies:
        one.start()
    empty = jnp.zeros((PADDED - QUART * UNITS, WIDTH), BF16)
    for end in (PADDED, 2 * PADDED):
        held_ref[end - PADDED + QUART * UNITS : end, :] = empty
    for one in copies:
        one.wait()


def expert_kernel(
    recv_ref, weight_ref, out_ref, tiles_ref, rows_ref, x_ref, held_ref, hidden_ref, sems, weight_sems
):
    arrivals = []
    for n in range(SLOTS // CHUNK):
        some = pl.ds(n * CHUNK, CHUNK)
        arrivals.append(pltpu.make_async_copy(recv_ref.at[some], tiles_ref.at[some], sems.at[n]))
    parts = []
    for n, (at, size) in enumerate(((0, 512), (512, 1024), (1536, 1536))):
        some = pl.ds(at, size)
        parts.append(
            pltpu.make_async_copy(weight_ref.at[some, :], held_ref.at[some, :], weight_sems.at[n])
        )
    for one in arrivals + parts:
        one.start()

    def unpack(t, carry):
        rows_ref[pl.ds(t * PITCH, HEADS), :] = tiles_ref[t].astype(F32)
        return carry

    for n in range(SLOTS // CHUNK):
        arrivals[n].wait()
        lax.fori_loop(n * CHUNK, (n + 1) * CHUNK, unpack, 0, unroll=16)
    for j in range(HEADS):
        x_ref[:, j * HEAD : (j + 1) * HEAD] = rows_ref[
            pl.ds(j, SLOTS, stride=PITCH), :
        ].astype(BF16)
    for part, blocks in ((0, (0, 1)), (1, (2, 3, 4, 5))):
        parts[part].wait()
        for n in blocks:
            here = slice(n * 256, (n + 1) * 256)
            hidden = 0.5 * dot(x_ref[...], held_ref[here, :], 1, 1)
            hidden_ref[:, here] = (hidden + hidden * jnp.tanh(hidden)).astype(BF16)
    parts[2].wait()

    def columns(n, carry):
        here = pl.ds(pl.multiple_of(n * 256, 256), 256)
        result = dot(hidden_ref[...], held_ref[PADDED:, here])
        rows_ref[pl.ds(2 * n, SLOTS, stride=PITCH), :] = result[:, :HEAD]
        rows_ref[pl.ds(2 * n + 1, SLOTS, stride=PITCH), :] = result[:, HEAD:]
        return carry

    lax.fori_loop(0, WIDTH // 256, columns, 0, unroll=4)

    def pack(t, carry):
        tiles_ref[t] = rows_ref[pl.ds(t * PITCH, HEADS), :].astype(BF16)
        return carry

    leaving = []
    for n in range(SLOTS // CHUNK):
        lax.fori_loop(n * CHUNK, (n + 1) * CHUNK, pack, 0, unroll=16)
        some = pl.ds(n * CHUNK, CHUNK)
        leaving.append(pltpu.make_async_copy(tiles_ref.at[some], out_ref.at[some], sems.at[n]))
        leaving[n].start()
    for one in leaving:
        one.wait()


def combine_kernel(slot_ref, gate_ref, back_ref, attn_ref, out_ref, rows_ref):
    def one(t, carry):
        moe = back_ref[slot_ref[2 * t]].astype(F32) * gate_ref[2 * t]
        moe = moe + back_ref[slot_ref[2 * t + 1]].astype(F32) * gate_ref[2 * t + 1]
        rows_ref[pl.ds(t * PITCH, HEADS), :] = attn_ref[t].astype(F32) + moe
        return carry

    lax.fori_loop(0, TOK, one, 0, unroll=8)
    for j in range(HEADS):
        out_ref[:, j * HEAD : (j + 1) * HEAD] = rows_ref[
            pl.ds(j, TOK, stride=PITCH), :
        ].astype(BF16)


VMEM = pl.BlockSpec(memory_space=pltpu.VMEM)
SMEM = pl.BlockSpec(memory_space=pltpu.SMEM)
FAR = pl.BlockSpec(memory_space=pltpu.HBM)


def call(kernel, outs, in_specs, scratch=(), flops=0, moved=0, exps=0, room=16, place=VMEM):
    shapes = [jax.ShapeDtypeStruct(shape, dtype) for shape, dtype in outs]
    return pl.pallas_call(
        kernel,
        out_shape=shapes if len(shapes) > 1 else shapes[0],
        in_specs=in_specs,
        out_specs=[place] * len(shapes) if len(shapes) > 1 else place,
        scratch_shapes=list(scratch),
        compiler_params=pltpu.CompilerParams(vmem_limit_bytes=room << 20),
        cost_estimate=pl.CostEstimate(flops=flops, bytes_accessed=moved, transcendentals=exps),
    )


def swapped(x, bit):
    peers = lax.axis_size("wide")
    return lax.ppermute(x, "wide", [(i, i ^ bit) for i in range(peers)])


def exchanged(x, axis):
    return lax.all_to_all(x, axis, split_axis=0, concat_axis=0, tiled=True)


def routed(rows):
    flat = rows.reshape(SLOTS * HEADS, HEAD)
    groups = [[e * QUART + q for e in range(EXPERTS)] for q in range(QUART)] if GROUPED else None
    traded = lax.all_to_all(
        flat, "wide", split_axis=0, concat_axis=0, tiled=True, axis_index_groups=groups
    )
    return traded.reshape(rows.shape)


def per_device(
    queries, key_tensor, value_tensor, decay_logarithm, lin_gain, routes, route_weight, w_up, w_down
):
    devices = lax.axis_size(BOTH)
    message, pair = call(
        state_kernel,
        [((devices, 128), F32), ((2 * TOK, KV * HEAD), BF16)],
        [VMEM] * 3,
        room=58,
        flops=1 << 24,
        moved=600_000,
    )(key_tensor, value_tensor, decay_logarithm)
    gathered = exchanged(message, BOTH)
    previous = lax.ppermute(pair, BOTH, [(i, i + 1) for i in range(devices - 1)])
    up = w_up.T
    plane = lax.axis_index("narrow").astype(jnp.int32).reshape(1)
    planes = lax.axis_size("narrow")
    piece = call(
        pick_kernel,
        [((PIECE, WIDTH), BF16)],
        [SMEM, FAR, FAR],
        [pltpu.SemaphoreType.DMA],
        room=58,
        moved=1_400_000,
    )(plane, up, w_down)
    pieces = [swapped(piece, 2)]
    for by in (1, 2, 3):
        around = [(i, (i + by) % planes) for i in range(planes)]
        pieces.append(lax.ppermute(pieces[0], "narrow", around))
    up_c, down_c = swapped(up, 1), swapped(w_down, 1)
    onward = [swapped(one, 1) for one in pieces]

    before = call(
        prefix_kernel, [((devices, 128), F32)], [VMEM], flops=1 << 22, moved=524_288
    )(gathered)
    before = exchanged(before, BOTH)

    flat = routes.reshape(-1)
    onehot = (flat[:, None] == jnp.arange(EXPERTS)[None, :]).astype(jnp.int32)
    rank = jnp.sum((jnp.cumsum(onehot, axis=0) - onehot) * onehot, axis=1)
    slots = flat * MOST + rank
    started = jnp.minimum(lax.axis_index(BOTH), 1).astype(jnp.int32).reshape(1)
    window, inner = call(
        local_kernel,
        [((TOK, WIDTH), F32)] * 2,
        [SMEM] + [VMEM] * 5,
        flops=1 << 29,
        moved=3_000_000,
        exps=1 << 18,
    )(started, queries, key_tensor, value_tensor, previous, decay_logarithm)
    attn, send = call(
        finish_kernel,
        [((TOK, HEADS, HEAD), BF16), ((SLOTS, HEADS, HEAD), BF16)],
        [SMEM] + [VMEM] * 6,
        [pltpu.VMEM((TOK * PITCH, HEAD), F32)],
        flops=1 << 28,
        moved=5_000_000,
    )(slots, queries, before, decay_logarithm, lin_gain.reshape(1, WIDTH), window, inner)

    received = routed(send)
    held = call(
        assemble_kernel,
        [((2 * PADDED, WIDTH), BF16)],
        [SMEM] + [FAR] * 12,
        [pltpu.SemaphoreType.DMA((12,))],
        room=62,
        moved=24_000_000,
    )(plane, up, w_down, up_c, down_c, *pieces, *onward)
    computed = call(
        expert_kernel,
        [((SLOTS, HEADS, HEAD), BF16)],
        [FAR] * 2,
        [
            pltpu.VMEM((SLOTS, HEADS, HEAD), BF16),
            pltpu.VMEM((SLOTS * PITCH, HEAD), F32),
            pltpu.VMEM((SLOTS, WIDTH), BF16),
            pltpu.VMEM((2 * PADDED, WIDTH), BF16),
            pltpu.VMEM((SLOTS, PADDED), BF16),
            pltpu.SemaphoreType.DMA((SLOTS // CHUNK,)),
            pltpu.SemaphoreType.DMA((3,)),
        ],
        room=62,
        place=FAR,
        flops=4_500_000_000,
        moved=15_000_000,
        exps=1 << 19,
    )(received, held)
    back = routed(computed)
    return call(
        combine_kernel,
        [((TOK, WIDTH), BF16)],
        [SMEM] * 2 + [VMEM] * 2,
        [pltpu.VMEM((TOK * PITCH, HEAD), F32)],
        flops=1 << 20,
        moved=2_600_000,
    )(slots, route_weight.reshape(-1), back, attn)


def solution(mesh):
    rows = P(("wide", "narrow"), None)
    in_specs = (rows, rows, rows, P(None, ("wide", "narrow")), P(), rows, rows, P(None, "wide"), P("wide", None))
    return jax.shard_map(per_device, mesh=mesh, in_specs=in_specs, out_specs=rows, check_vma=False)
```

```python
import jax
import jax.numpy as jnp
from jax import lax
from jax.experimental import pallas as pl
from jax.experimental.pallas import tpu as pltpu
from jax.sharding import PartitionSpec as P


EXPERTS = 32
QUART = 4
MOST = 12
TOK = 128
HEADS = 16
HEAD = 128
KV = 2
GROUP = HEADS // KV
WIDTH = HEADS * HEAD
UNITS = 352
PADDED = 1536
PIECE = 176
PITCH = 17
CHUNK = 96
SLOTS = EXPERTS * MOST
SCALE = HEAD ** (-0.5)
BOTH = ("wide", "narrow")
F32 = jnp.float32
BF16 = jnp.bfloat16
GROUPED = True


def dot(a, b, lhs=1, rhs=0):
    return lax.dot_general(a, b, (((lhs,), (rhs,)), ((), ())), preferred_element_type=F32)


def iota(shape, dim):
    return lax.broadcasted_iota(jnp.int32, shape, dim)


def split(x):
    high = x.astype(BF16)
    return high, (x - high.astype(F32)).astype(BF16)


def decay_sums(decay_ref, head):
    total = jnp.broadcast_to(decay_ref[head : head + 1, :], (8, TOK))
    lane = iota((8, TOK), 1)
    for by in (1, 2, 4, 8, 16, 32, 64):
        total = total + jnp.where(lane >= by, pltpu.roll(total, by, 1), 0.0)
    row = jnp.broadcast_to(total[0:1, :], (TOK, TOK))
    same = iota((TOK, TOK), 0) == iota((TOK, TOK), 1)
    column = jnp.sum(jnp.where(same, row, 0.0), axis=1, keepdims=True)
    return row, column


def state_kernel(key_ref, value_ref, decay_ref, message_ref, pair_ref):
    lane = iota((HEAD, HEAD), 1)
    for head in range(KV):
        cols = slice(head * HEAD, (head + 1) * HEAD)
        row, column = decay_sums(decay_ref, head)
        last = row[:, TOK - 1 : TOK]
        weighted = key_ref[:, cols].astype(F32) * jnp.exp(last - column)
        high, low = split(weighted)
        values = value_ref[:, cols]
        state = dot(
            jnp.concatenate([high, low], axis=0), jnp.concatenate([values, values], axis=0), 0, 0
        )
        fade = jnp.exp(jnp.broadcast_to(last, (HEAD, HEAD)))
        message_ref[head * HEAD : (head + 1) * HEAD, :] = jnp.where(lane < 64, state, fade)
        message_ref[256 + head * HEAD : 256 + (head + 1) * HEAD, :] = jnp.where(
            lane < 64, pltpu.roll(state, 64, 1), fade
        )
    pair_ref[:TOK, :] = key_ref[...]
    pair_ref[TOK:, :] = value_ref[...]


def prefix_kernel(message_ref, before_ref):
    count = message_ref.shape[0]
    shape = (count, 128)
    first = iota(shape, 1) < 64
    place = iota(shape, 0)
    neutral = jnp.where(first, 0.0, 1.0)
    run = message_ref[...]
    by = 1
    while by < count:
        earlier = jnp.where(place >= by, pltpu.roll(run, by, 0), neutral)
        fade = jnp.where(first, pltpu.roll(run, 64, 1), run)
        run = earlier * fade + jnp.where(first, run, 0.0)
        by *= 2
    before_ref[...] = jnp.where(place >= 1, pltpu.roll(run, 1, 0), 0.0)


def local_kernel(
    started_ref, query_ref, key_ref, value_ref, prev_ref, decay_ref, window_ref, inner_ref
):
    seen = iota((TOK, TOK), 1) <= iota((TOK, TOK), 0)
    usable = jnp.logical_or(seen, jnp.broadcast_to(started_ref[0] > 0, (TOK, TOK)))
    for head in range(KV):
        cols = slice(head * HEAD, (head + 1) * HEAD)
        row, column = decay_sums(decay_ref, head)
        weight = jnp.where(seen, jnp.exp(jnp.where(seen, column - row, 0.0)), 0.0)
        keys = jnp.concatenate([key_ref[:, cols], prev_ref[:TOK, cols]], axis=0)
        own = value_ref[:, cols]
        values = jnp.concatenate([own, prev_ref[TOK:, cols]], axis=0)
        twice = jnp.concatenate([own, own], axis=0)

        def one(j, carry):
            here = pl.ds(pl.multiple_of((head * GROUP + j) * HEAD, HEAD), HEAD)
            scores = dot(query_ref[:, here], keys, 1, 1)
            now, prev = scores[:, :TOK], scores[:, TOK:]
            high, low = split(now * weight)
            inner_ref[:, here] = dot(jnp.concatenate([high, low], axis=1), twice)
            masked = jnp.where(usable, jnp.where(seen, now, prev) * SCALE, -jnp.inf)
            expo = jnp.exp(masked - jnp.max(masked, axis=1, keepdims=True))
            probs = expo / jnp.sum(expo, axis=1, keepdims=True)
            both = jnp.concatenate(
                [jnp.where(seen, probs, 0.0), jnp.where(seen, 0.0, probs)], axis=1
            )
            window_ref[:, here] = dot(both.astype(BF16), values)
            return carry

        lax.fori_loop(0, GROUP, one, 0, unroll=8)


def finish_kernel(
    slot_ref, query_ref, before_ref, decay_ref, gain_ref, window_ref, inner_ref, attn_ref, send_ref, rows_ref
):
    lane = iota((HEAD, HEAD), 1)
    send_ref[...] = jnp.zeros(send_ref.shape, BF16)
    for head in range(KV):
        _, column = decay_sums(decay_ref, head)
        left = before_ref[head * HEAD : (head + 1) * HEAD, :]
        right = before_ref[256 + head * HEAD : 256 + (head + 1) * HEAD, :]
        state = jnp.where(lane < 64, left, pltpu.roll(right, 64, 1))
        halves = jnp.concatenate(split(state), axis=1)
        fade = jnp.exp(column)

        def one(j, carry):
            number = head * GROUP + j
            here = pl.ds(pl.multiple_of(number * HEAD, HEAD), HEAD)
            product = dot(query_ref[:, here], halves)
            carried = (product[:, :HEAD] + product[:, HEAD:]) * fade
            linear = (carried + inner_ref[:, here]) * SCALE
            mean = jnp.mean(linear * linear, axis=1, keepdims=True)
            normed = linear / jnp.sqrt(mean + 1e-06) * gain_ref[:, here]
            rows_ref[pl.ds(number, TOK, stride=PITCH), :] = normed + window_ref[:, here]
            return carry

        lax.fori_loop(0, GROUP, one, 0, unroll=8)

    def place(t, carry):
        row = rows_ref[pl.ds(t * PITCH, HEADS), :].astype(BF16)
        attn_ref[t] = row
        send_ref[slot_ref[2 * t]] = row
        send_ref[slot_ref[2 * t + 1]] = row
        return carry

    lax.fori_loop(0, TOK, place, 0, unroll=32)


def pick_kernel(plane_ref, up_ref, down_ref, piece_ref, sem):
    plane = plane_ref[0]
    rows = pl.ds(pl.multiple_of(lax.rem(plane, 2) * PIECE, PIECE), PIECE)

    @pl.when(plane < 2)
    def from_up():
        pltpu.make_async_copy(up_ref.at[rows, :], piece_ref, sem).start()

    @pl.when(plane >= 2)
    def from_down():
        pltpu.make_async_copy(down_ref.at[rows, :], piece_ref, sem).start()

    pltpu.make_async_copy(down_ref.at[rows, :], piece_ref, sem).wait()


def assemble_kernel(plane_ref, *refs):
    sources, (held_ref, sems) = refs[:12], refs[12:]
    plane = plane_ref[0]
    copies = []
    for n, at in enumerate((0, PADDED, UNITS, PADDED + UNITS)):
        copies.append(
            pltpu.make_async_copy(sources[n], held_ref.at[pl.ds(at, UNITS), :], sems.at[n])
        )
    for n in range(8):
        shard, step = n // 4, n % 4
        quarter = lax.rem(plane - step + 4, 4)
        at = (2 + shard) * UNITS + lax.rem(quarter, 2) * PIECE
        at = at + jnp.where(quarter < 2, 0, PADDED)
        place = pl.ds(pl.multiple_of(at, PIECE // 11), PIECE)
        copies.append(
            pltpu.make_async_copy(sources[4 + n], held_ref.at[place, :], sems.at[4 + n])
        )
    for one in copies:
        one.start()
    empty = jnp.zeros((PADDED - QUART * UNITS, WIDTH), BF16)
    for end in (PADDED, 2 * PADDED):
        held_ref[end - PADDED + QUART * UNITS : end, :] = empty
    for one in copies:
        one.wait()


def expert_kernel(
    recv_ref, weight_ref, out_ref, tiles_ref, rows_ref, x_ref, held_ref, hidden_ref, sems, weight_sems
):
    arrivals = []
    for n in range(SLOTS // CHUNK):
        some = pl.ds(n * CHUNK, CHUNK)
        arrivals.append(pltpu.make_async_copy(recv_ref.at[some], tiles_ref.at[some], sems.at[n]))
    parts = []
    for n, (at, size) in enumerate(((0, 512), (512, 1024), (1536, 1536))):
        some = pl.ds(at, size)
        parts.append(
            pltpu.make_async_copy(weight_ref.at[some, :], held_ref.at[some, :], weight_sems.at[n])
        )
    for one in arrivals + parts:
        one.start()

    def unpack(t, carry):
        rows_ref[pl.ds(t * PITCH, HEADS), :] = tiles_ref[t].astype(F32)
        return carry

    for n in range(SLOTS // CHUNK):
        arrivals[n].wait()
        lax.fori_loop(n * CHUNK, (n + 1) * CHUNK, unpack, 0, unroll=CHUNK)
    for j in range(HEADS):
        x_ref[:, j * HEAD : (j + 1) * HEAD] = rows_ref[
            pl.ds(j, SLOTS, stride=PITCH), :
        ].astype(BF16)
    for part, blocks in ((0, (0, 1)), (1, (2, 3, 4, 5))):
        parts[part].wait()
        for n in blocks:
            here = slice(n * 256, (n + 1) * 256)
            hidden = 0.5 * dot(x_ref[...], held_ref[here, :], 1, 1)
            hidden_ref[:, here] = (hidden + hidden * jnp.tanh(hidden)).astype(BF16)
    parts[2].wait()

    def columns(n, carry):
        here = pl.ds(pl.multiple_of(n * 256, 256), 256)
        result = dot(hidden_ref[...], held_ref[PADDED:, here])
        rows_ref[pl.ds(2 * n, SLOTS, stride=PITCH), :] = result[:, :HEAD]
        rows_ref[pl.ds(2 * n + 1, SLOTS, stride=PITCH), :] = result[:, HEAD:]
        return carry

    lax.fori_loop(0, WIDTH // 256, columns, 0, unroll=4)

    def pack(t, carry):
        tiles_ref[t] = rows_ref[pl.ds(t * PITCH, HEADS), :].astype(BF16)
        return carry

    leaving = []
    for n in range(SLOTS // CHUNK):
        lax.fori_loop(n * CHUNK, (n + 1) * CHUNK, pack, 0, unroll=CHUNK)
        some = pl.ds(n * CHUNK, CHUNK)
        leaving.append(pltpu.make_async_copy(tiles_ref.at[some], out_ref.at[some], sems.at[n]))
        leaving[n].start()
    for one in leaving:
        one.wait()


def combine_kernel(slot_ref, gate_ref, back_ref, attn_ref, out_ref, rows_ref):
    def one(t, carry):
        moe = back_ref[slot_ref[2 * t]].astype(F32) * gate_ref[2 * t]
        moe = moe + back_ref[slot_ref[2 * t + 1]].astype(F32) * gate_ref[2 * t + 1]
        rows_ref[pl.ds(t * PITCH, HEADS), :] = attn_ref[t].astype(F32) + moe
        return carry

    lax.fori_loop(0, TOK, one, 0, unroll=32)
    for j in range(HEADS):
        out_ref[:, j * HEAD : (j + 1) * HEAD] = rows_ref[
            pl.ds(j, TOK, stride=PITCH), :
        ].astype(BF16)


VMEM = pl.BlockSpec(memory_space=pltpu.VMEM)
SMEM = pl.BlockSpec(memory_space=pltpu.SMEM)
FAR = pl.BlockSpec(memory_space=pltpu.HBM)


def call(kernel, outs, in_specs, scratch=(), flops=0, moved=0, exps=0, room=16, place=VMEM):
    shapes = [jax.ShapeDtypeStruct(shape, dtype) for shape, dtype in outs]
    return pl.pallas_call(
        kernel,
        out_shape=shapes if len(shapes) > 1 else shapes[0],
        in_specs=in_specs,
        out_specs=[place] * len(shapes) if len(shapes) > 1 else place,
        scratch_shapes=list(scratch),
        compiler_params=pltpu.CompilerParams(vmem_limit_bytes=room << 20),
        cost_estimate=pl.CostEstimate(flops=flops, bytes_accessed=moved, transcendentals=exps),
    )


def swapped(x, bit):
    peers = lax.axis_size("wide")
    return lax.ppermute(x, "wide", [(i, i ^ bit) for i in range(peers)])


def exchanged(x, axis):
    return lax.all_to_all(x, axis, split_axis=0, concat_axis=0, tiled=True)


def routed(rows):
    flat = rows.reshape(SLOTS * HEADS, HEAD)
    groups = [[e * QUART + q for e in range(EXPERTS)] for q in range(QUART)] if GROUPED else None
    traded = lax.all_to_all(
        flat, "wide", split_axis=0, concat_axis=0, tiled=True, axis_index_groups=groups
    )
    return traded.reshape(rows.shape)


def per_device(
    queries, key_tensor, value_tensor, decay_logarithm, lin_gain, routes, route_weight, w_up, w_down
):
    devices = lax.axis_size(BOTH)
    message, pair = call(
        state_kernel,
        [((devices, 128), F32), ((2 * TOK, KV * HEAD), BF16)],
        [VMEM] * 3,
        room=58,
        flops=1 << 24,
        moved=600_000,
    )(key_tensor, value_tensor, decay_logarithm)
    gathered = exchanged(message, BOTH)
    previous = lax.ppermute(pair, BOTH, [(i, i + 1) for i in range(devices - 1)])
    up = w_up.T
    plane = lax.axis_index("narrow").astype(jnp.int32).reshape(1)
    planes = lax.axis_size("narrow")
    piece = call(
        pick_kernel,
        [((PIECE, WIDTH), BF16)],
        [SMEM, FAR, FAR],
        [pltpu.SemaphoreType.DMA],
        room=58,
        moved=1_400_000,
    )(plane, up, w_down)
    pieces = [swapped(piece, 2)]
    for by in (1, 2, 3):
        around = [(i, (i + by) % planes) for i in range(planes)]
        pieces.append(lax.ppermute(pieces[0], "narrow", around))
    up_c, down_c = swapped(up, 1), swapped(w_down, 1)
    onward = [swapped(one, 1) for one in pieces]

    before = call(
        prefix_kernel, [((devices, 128), F32)], [VMEM], flops=1 << 22, moved=524_288
    )(gathered)
    before = exchanged(before, BOTH)

    flat = routes.reshape(-1)
    onehot = (flat[:, None] == jnp.arange(EXPERTS)[None, :]).astype(jnp.int32)
    rank = jnp.sum((jnp.cumsum(onehot, axis=0) - onehot) * onehot, axis=1)
    slots = flat * MOST + rank
    started = jnp.minimum(lax.axis_index(BOTH), 1).astype(jnp.int32).reshape(1)
    window, inner = call(
        local_kernel,
        [((TOK, WIDTH), F32)] * 2,
        [SMEM] + [VMEM] * 5,
        flops=1 << 29,
        moved=3_000_000,
        exps=1 << 18,
    )(started, queries, key_tensor, value_tensor, previous, decay_logarithm)
    attn, send = call(
        finish_kernel,
        [((TOK, HEADS, HEAD), BF16), ((SLOTS, HEADS, HEAD), BF16)],
        [SMEM] + [VMEM] * 6,
        [pltpu.VMEM((TOK * PITCH, HEAD), F32)],
        flops=1 << 28,
        moved=5_000_000,
    )(slots, queries, before, decay_logarithm, lin_gain.reshape(1, WIDTH), window, inner)

    received = routed(send)
    held = call(
        assemble_kernel,
        [((2 * PADDED, WIDTH), BF16)],
        [SMEM] + [FAR] * 12,
        [pltpu.SemaphoreType.DMA((12,))],
        room=44,
        moved=24_000_000,
    )(plane, up, w_down, up_c, down_c, *pieces, *onward)
    computed = call(
        expert_kernel,
        [((SLOTS, HEADS, HEAD), BF16)],
        [FAR] * 2,
        [
            pltpu.VMEM((SLOTS, HEADS, HEAD), BF16),
            pltpu.VMEM((SLOTS * PITCH, HEAD), F32),
            pltpu.VMEM((SLOTS, WIDTH), BF16),
            pltpu.VMEM((2 * PADDED, WIDTH), BF16),
            pltpu.VMEM((SLOTS, PADDED), BF16),
            pltpu.SemaphoreType.DMA((SLOTS // CHUNK,)),
            pltpu.SemaphoreType.DMA((3,)),
        ],
        room=62,
        place=FAR,
        flops=4_500_000_000,
        moved=15_000_000,
        exps=1 << 19,
    )(received, held)
    back = routed(computed)
    return call(
        combine_kernel,
        [((TOK, WIDTH), BF16)],
        [SMEM] * 2 + [VMEM] * 2,
        [pltpu.VMEM((TOK * PITCH, HEAD), F32)],
        flops=1 << 20,
        moved=2_600_000,
    )(slots, route_weight.reshape(-1), back, attn)


def solution(mesh):
    rows = P(("wide", "narrow"), None)
    in_specs = (rows, rows, rows, P(None, ("wide", "narrow")), P(), rows, rows, P(None, "wide"), P("wide", None))
    return jax.shard_map(per_device, mesh=mesh, in_specs=in_specs, out_specs=rows, check_vma=False)
```
